128 devices in a mesh: row: 8 (over y, x_hi), col: 16 (over x_lo, z, core).
Axes of the slice: x: 4 (x_hi: 2, x_lo: 2; x = x_hi * 2 + x_lo), y: 4, z: 4, core: 2. Of those that a mesh axis runs over, the one named last changes fastest.
Arguments:
- cov: float32 [8192, 8192], P('row', 'col'), as said below
- obs_cells: int32 [3, 256], replicated, may hold values from 0 to 8191, as said below
- obs_var: float32 [3, 256], replicated, may hold values from 0.25 to 1
- wind: float32 [2, 64, 128], replicated, may hold values from -0.2 to 0.2
- diffusivity: float32 [64, 128], replicated, may hold values from 0.01 to 0.05
- noise: float32 [64, 128], replicated, may hold values from 0.05 to 0.5
Outputs:
- forecast: float32 [8192, 8192], P('row', 'col')
The draws below stay inside these ranges and needn't reach their ends.
Inputs may be any that keep to these rules, and one draw needn't show every extreme that they name: `cov`: symmetric and positive definite. `obs_cells`: within each batch the 256 cells are distinct, and every batch observes cell 0 and cell 8192 - 1.
All inputs are finite; a program needn't handle non-finite values.
Results may differ from the reference program's by a relative error of at most 0.00013.
Values sent between devices are 32-bit elements; how exact they have to be, the bound alone decides.
No kernel may reach another device: no remote copies, remote signals or barrier semaphores. Data moves between devices by JAX's collectives and lax.ppermute only.
A program may use at most 64 MiB of HBM per device.

```python
import math
import jax
import jax.numpy as jnp
from jax import lax

GRID_W = 128
NOBS = 256
BATCHES = 3
FSTEPS = 2
GRID_ROWS = 64
NCELL = 8192


def draw_cov(key, part):
    cells = GRID_ROWS * GRID_W
    first, second, third, fourth = jax.random.split(key, 4)
    positions = jnp.arange(cells, dtype=jnp.int32)
    grid_y = (positions // GRID_W).astype(jnp.float32)
    grid_x = (positions % GRID_W).astype(jnp.float32)
    matrix = jax.random.normal(first, (cells, cells), jnp.float32)
    sigma = jnp.exp(jax.random.uniform(second, (cells,), jnp.float32, jnp.log(1.0), jnp.log(2.0)))
    nugget = jnp.exp(jax.random.uniform(third, (cells,), jnp.float32, jnp.log(1.0), jnp.log(2.0)))
    length = jax.random.uniform(fourth, (), jnp.float32, 4.0, 10.0)
    delta_y = grid_y[:, None] - grid_y[None, :]
    delta_x = grid_x[:, None] - grid_x[None, :]
    distance = jnp.sqrt(delta_y * delta_y + delta_x * delta_x)
    kernel = sigma[:, None] * sigma[None, :] * jnp.exp(-distance / length)
    symmetric = (matrix + matrix.T) * (0.25 / jnp.sqrt(jnp.float32(cells)))
    return (kernel + symmetric).at[positions, positions].add(nugget)


def draw_obs_cells(key, part):
    cells = GRID_ROWS * GRID_W
    subkeys = jax.random.split(key, BATCHES)

    def single(subkey):
        first, second = jax.random.split(subkey)
        inner = jax.random.permutation(first, cells - 2)[:NOBS - 2].astype(jnp.int32) + 1
        chosen = jnp.concatenate([inner, jnp.array([0, cells - 1], jnp.int32)])
        return chosen[jax.random.permutation(second, NOBS)]
    return jax.vmap(single)(subkeys).astype(jnp.int32)


def setup_inputs(seed: int = 0) -> dict:
    streams_of = jax.random.split(jax.random.key(seed), 7)
    cov = draw_cov(jax.random.fold_in(streams_of[6], 71), 0)
    obs_cells = draw_obs_cells(jax.random.fold_in(streams_of[6], 71), 0)
    obs_var = jnp.clip(jnp.exp(jax.random.uniform(streams_of[2], (BATCHES, NOBS), jnp.float32, math.log(0.25), math.log(1.0))), 0.25, 1.0)
    wind = jnp.clip(jax.random.uniform(streams_of[3], (2, GRID_ROWS, GRID_W), jnp.float32, -0.2, 0.2), -0.2, 0.2)
    diffusivity = jnp.clip(jnp.exp(jax.random.uniform(streams_of[4], (GRID_ROWS, GRID_W), jnp.float32, math.log(0.01), math.log(0.05))), 0.01, 0.05)
    noise = jnp.clip(jnp.exp(jax.random.uniform(streams_of[5], (GRID_ROWS, GRID_W), jnp.float32, math.log(0.05), math.log(0.5))), 0.05, 0.5)
    return dict(cov=cov, obs_cells=obs_cells, obs_var=obs_var, wind=wind, diffusivity=diffusivity, noise=noise)


def stencil_table(wind, diffusivity):
    east_wind = wind[0]
    north_wind = wind[1]
    from_west = diffusivity + jnp.maximum(east_wind, 0.0)
    from_east = diffusivity + jnp.maximum(-east_wind, 0.0)
    from_north = diffusivity + jnp.maximum(north_wind, 0.0)
    from_south = diffusivity + jnp.maximum(-north_wind, 0.0)
    center = 1.0 - (from_west + from_east + from_north + from_south)
    return jnp.stack([center, from_west, from_east, from_north, from_south]).reshape(5, -1)

def along_rows(block, weights, width):
    count = block.shape[0] // width
    cube = block.reshape(count, width, block.shape[1])
    coef = weights.reshape(5, count, width, 1)
    padded = jnp.pad(cube, ((1, 1), (1, 1), (0, 0)))
    result = coef[0] * cube + coef[1] * padded[1:-1, :-2] + coef[2] * padded[1:-1, 2:] + coef[3] * padded[:-2, 1:-1] + coef[4] * padded[2:, 1:-1]
    return result.reshape(block.shape)

def along_cols(block, weights, width):
    count = block.shape[1] // width
    cube = block.reshape(block.shape[0], count, width)
    coef = weights.reshape(5, 1, count, width)
    padded = jnp.pad(cube, ((0, 0), (1, 1), (1, 1)))
    result = coef[0] * cube + coef[1] * padded[:, 1:-1, :-2] + coef[2] * padded[:, 1:-1, 2:] + coef[3] * padded[:, :-2, 1:-1] + coef[4] * padded[:, 2:, 1:-1]
    return result.reshape(block.shape)

def reference(cov, obs_cells, obs_var, wind, diffusivity, noise):
    highest = lax.Precision.HIGHEST
    for batch_index in range(BATCHES):
        cells = obs_cells[batch_index]
        picked_rows = cov[cells, :]
        picked_cols = cov[:, cells]
        innovation = picked_rows[:, cells] + jnp.diag(obs_var[batch_index])
        factor = jnp.linalg.cholesky(innovation)
        halfway = lax.linalg.triangular_solve(factor, picked_rows, left_side=True, lower=True)
        solved = lax.linalg.triangular_solve(factor, halfway, left_side=True, lower=True, transpose_a=True)
        cov = cov - jnp.dot(picked_cols.astype(jnp.float32), solved.astype(jnp.float32), precision=highest, preferred_element_type=jnp.float32)
    table = stencil_table(wind, diffusivity)
    flat_noise = noise.reshape(-1)
    diagonal_index = jnp.arange(NCELL, dtype=jnp.int32)
    for step in range(FSTEPS):
        cov = along_rows(cov, table, GRID_W)
        cov = along_cols(cov, table, GRID_W)
        cov = cov.at[diagonal_index, diagonal_index].add(flat_noise)
    return cov
```

```python
import functools

import jax
import jax.numpy as jnp
from jax import lax
from jax.experimental import pallas as pl
from jax.experimental.pallas import tpu as pltpu
from jax.sharding import PartitionSpec as P

HI = lax.Precision.HIGHEST
F32 = jnp.float32
W = 128
ROWS = 8
COLS = 16


def dot(a, b, dims=((1,), (0,)), precision=HI):
    return lax.dot_general(a, b, (dims, ((), ())), precision=precision, preferred_element_type=F32)


def recip(x):
    r = pl.reciprocal(x, approx=True)
    r = r * (2.0 - x * r)
    return r * (2.0 - x * r)


def lane_b(v, lane):
    return jnp.broadcast_to(v[:, lane : lane + 1], (8, 128))


def sub_b(v, sub):
    return jnp.broadcast_to(v[sub : sub + 1, :], (8, 128))


def invert_block(rows):
    lane = lax.broadcasted_iota(jnp.int32, (8, 128), 1)
    sub = lax.broadcasted_iota(jnp.int32, (8, 128), 0)
    rows = list(rows)
    for p in range(16):
        base = 8 * p
        panel = (lane >= base) & (lane < base + 8)
        src = rows[p]
        rb = [sub_b(src, i) for i in range(8)]
        e = [[lane_b(rb[i], base + j) for j in range(8)] for i in range(8)]
        rb = [jnp.where(panel, jnp.where(lane == base + i, 1.0, 0.0), rb[i]) for i in range(8)]
        for k in range(8):
            r = recip(e[k][k])
            for j in range(k + 1, 8):
                e[k][j] = e[k][j] * r
            rb[k] = rb[k] * r
            for i in range(8):
                if i == k:
                    continue
                f = e[i][k]
                for j in range(k + 1, 8):
                    e[i][j] = e[i][j] - f * e[k][j]
                rb[i] = rb[i] - f * rb[k]
        for q in list(range(p + 1, 16)) + list(range(p)):
            t = rows[q]
            even = jnp.where(panel, 0.0, t)
            odd = None
            for j in range(8):
                m = lane_b(t, base + j) * rb[j]
                if j % 2 == 0:
                    even = even - m
                else:
                    odd = m if odd is None else odd + m
            rows[q] = even - odd
        out = rb[0]
        for i in range(1, 8):
            out = jnp.where(sub == i, rb[i], out)
        rows[p] = out
    return rows


def inverse_kernel(s_ref, o_ref, d_ref, y_ref, *, n):
    o_ref[...] = s_ref[...]

    def body(kb, carry):
        off = pl.multiple_of(kb * 128, 128)
        blk = pl.ds(off, 128)
        rows = [o_ref[pl.ds(pl.multiple_of(off + 8 * q, 8), 8), blk] for q in range(16)]
        rows = invert_block(rows)
        for q in range(16):
            d_ref[8 * q : 8 * q + 8, :] = rows[q]
        dinv = d_ref[...]
        y_ref[...] = jnp.dot(dinv, o_ref[blk, :], precision=HI, preferred_element_type=F32)
        y_ref[:, blk] = dinv
        col = o_ref[:, blk]
        o_ref[:, blk] = jnp.zeros((n, 128), F32)
        o_ref[...] = o_ref[...] - jnp.dot(col, y_ref[...], precision=HI, preferred_element_type=F32)
        o_ref[blk, :] = y_ref[...]
        return carry

    lax.fori_loop(0, n // 128, body, 0)


def inverse(s):
    n = s.shape[0]
    return pl.pallas_call(
        functools.partial(inverse_kernel, n=n),
        out_shape=jax.ShapeDtypeStruct((n, n), F32),
        in_specs=[pl.BlockSpec(memory_space=pltpu.VMEM)],
        out_specs=pl.BlockSpec(memory_space=pltpu.VMEM),
        scratch_shapes=[pltpu.VMEM((128, 128), F32), pltpu.VMEM((128, n), F32)],
        name="inverse",
    )(s)


def stencil_table(wind, diffusivity):
    east_wind = wind[0]
    north_wind = wind[1]
    from_west = diffusivity + jnp.maximum(east_wind, 0.0)
    from_east = diffusivity + jnp.maximum(-east_wind, 0.0)
    from_north = diffusivity + jnp.maximum(north_wind, 0.0)
    from_south = diffusivity + jnp.maximum(-north_wind, 0.0)
    center = 1.0 - (from_west + from_east + from_north + from_south)
    return jnp.stack([center, from_west, from_east, from_north, from_south]).reshape(5, -1)


def along_rows(block, weights):
    count = block.shape[0] // W
    cube = block.reshape(count, W, block.shape[1])
    coef = weights.reshape(5, count, W, 1)
    padded = jnp.pad(cube, ((1, 1), (1, 1), (0, 0)))
    result = (
        coef[0] * cube
        + coef[1] * padded[1:-1, :-2]
        + coef[2] * padded[1:-1, 2:]
        + coef[3] * padded[:-2, 1:-1]
        + coef[4] * padded[2:, 1:-1]
    )
    return result.reshape(block.shape)


def along_cols(block, weights):
    count = block.shape[1] // W
    cube = block.reshape(block.shape[0], count, W)
    coef = weights.reshape(5, 1, count, W)
    padded = jnp.pad(cube, ((0, 0), (1, 1), (1, 1)))
    result = (
        coef[0] * cube
        + coef[1] * padded[:, 1:-1, :-2]
        + coef[2] * padded[:, 1:-1, 2:]
        + coef[3] * padded[:, :-2, 1:-1]
        + coef[4] * padded[:, 2:, 1:-1]
    )
    return result.reshape(block.shape)


def halos(block, axis, dim, width):
    count = lax.axis_size(axis)
    forward = [(i, i + 1) for i in range(count - 1)]
    backward = [(target, source) for source, target in forward]
    low = lax.ppermute(
        lax.slice_in_dim(block, block.shape[dim] - width, None, axis=dim), axis, forward
    )
    high = lax.ppermute(lax.slice_in_dim(block, 0, width, axis=dim), axis, backward)
    return jnp.concatenate([low, block, high], axis=dim)


def twice_cols(block, axis, weights):
    wide = halos(block, axis, 1, 2 * W)
    wide = along_cols(along_cols(wide, weights), weights)
    return wide[:, 2 * W : -2 * W]


def gather_sum(parts, axis, groups=None):
    count = lax.axis_size(axis)
    size = parts.shape[0] // count
    pieces = lax.all_to_all(parts.reshape(count, size, -1), axis, 0, 0)
    mine = jnp.sum(pieces, axis=0)
    full = lax.all_to_all(jnp.broadcast_to(mine[None], (count,) + mine.shape), axis, 0, 0)
    return full.reshape(parts.shape)


def local(cov, obs_cells, obs_var, wind, diffusivity, noise):
    rows_here, cols_here = cov.shape
    row_start = lax.axis_index("row") * rows_here
    col_start = lax.axis_index("col") * cols_here
    cells = obs_cells.reshape(-1)
    variances = obs_var.reshape(-1)
    nobs = cells.shape[0]

    margin = 2 * W
    table = jnp.pad(stencil_table(wind, diffusivity), ((0, 0), (margin, margin)))
    noise_padded = jnp.pad(noise.reshape(-1), (margin, margin))
    row_w = lax.dynamic_slice_in_dim(table, row_start, rows_here + 2 * margin, 1)
    col_w = lax.dynamic_slice_in_dim(table, col_start, cols_here + 2 * margin, 1)

    local_rows = cells - row_start
    row_hit = (local_rows >= 0) & (local_rows < rows_here)
    x_part = jnp.where(row_hit[:, None], cov[jnp.clip(local_rows, 0, rows_here - 1), :], 0.0)
    x = gather_sum(x_part, "row")
    local_cols = cells - col_start
    col_pick = (local_cols[:, None] == jnp.arange(cols_here, dtype=jnp.int32)[None, :]).astype(F32)
    y = gather_sum(dot(col_pick, cov, ((1,), (1,))), "col")
    corner = gather_sum(dot(x, col_pick, ((1,), (1,))), "col")
    inv = inverse(corner + jnp.diag(variances))

    vx = twice_cols(x, "col", col_w)
    vy = twice_cols(y, "row", row_w)

    tall = halos(cov, "row", 0, 2 * W)
    tall = along_rows(along_rows(tall, row_w), row_w)[2 * W : -2 * W]
    wide = halos(tall, "col", 1, 2 * W)
    wide = along_cols(wide, col_w)
    here = row_w[:, margin:-margin]
    row_ids = row_start + jnp.arange(rows_here, dtype=jnp.int32)
    col_ids = col_start - margin + jnp.arange(cols_here + 2 * margin, dtype=jnp.int32)
    noise_cols = lax.dynamic_slice_in_dim(noise_padded, col_start, cols_here + 2 * margin)
    gap = col_ids[None, :] - row_ids[:, None]
    grid_x = row_ids % W
    spread = jnp.where(gap == 0, here[0][:, None], 0.0)
    spread = jnp.where(gap == -1, jnp.where(grid_x > 0, here[1], 0.0)[:, None], spread)
    spread = jnp.where(gap == 1, jnp.where(grid_x < W - 1, here[2], 0.0)[:, None], spread)
    spread = jnp.where(gap == -W, here[3][:, None], spread)
    spread = jnp.where(gap == W, here[4][:, None], spread)
    wide = wide + spread * noise_cols[None, :]
    prior = along_cols(wide, col_w)[:, margin:-margin]
    noise_here = noise_cols[margin:-margin]
    gap_here = gap[:, margin:-margin]
    prior = prior + jnp.where(gap_here == 0, noise_here[None, :], 0.0)

    gain = dot(inv, vx)
    return prior - dot(vy, gain, ((0,), (0,)))


def solution(mesh):
    placed = (P("row", "col"), P(), P(), P(), P(), P())
    return jax.shard_map(
        local, mesh=mesh, in_specs=placed, out_specs=P("row", "col"), check_vma=False
    )
```

```python
import functools

import jax
import jax.numpy as jnp
from jax import lax
from jax.experimental import pallas as pl
from jax.experimental.pallas import tpu as pltpu
from jax.sharding import PartitionSpec as P


HI = lax.Precision.HIGHEST
F32 = jnp.float32
W = 128
ROWS = 8
COLS = 16
CAP_ROW = 128
CAP_COL = 72


def dot(a, b, dims=((1,), (0,)), precision=HI):
    return lax.dot_general(a, b, (dims, ((), ())), precision=precision, preferred_element_type=F32)


def recip(x):
    r = pltpu.reciprocal(x, approx=True)
    return r * (2.0 - x * r)


def lane_b(v, lane):
    return jnp.broadcast_to(v[:, lane : lane + 1], (8, 128))


def sub_b(v, sub):
    return jnp.broadcast_to(v[sub : sub + 1, :], (8, 128))


def invert_block(rows):
    lane = lax.broadcasted_iota(jnp.int32, (8, 128), 1)
    sub = lax.broadcasted_iota(jnp.int32, (8, 128), 0)
    rows = list(rows)
    for p in range(16):
        base = 8 * p
        panel = (lane >= base) & (lane < base + 8)
        src = rows[p]
        rb = [sub_b(src, i) for i in range(8)]
        e = [[lane_b(rb[i], base + j) if j >= i else None for j in range(8)] for i in range(8)]
        rb = [jnp.where(panel, jnp.where(lane == base + i, 1.0, 0.0), rb[i]) for i in range(8)]
        for k in range(8):
            r = recip(e[k][k])
            f = [e[i][k] if i < k else e[k][i] for i in range(8)]
            for j in range(k + 1, 8):
                e[k][j] = e[k][j] * r
            rb[k] = rb[k] * r
            for i in range(8):
                if i == k:
                    continue
                for j in range(max(i, k + 1), 8):
                    e[i][j] = e[i][j] - f[i] * e[k][j]
                rb[i] = rb[i] - f[i] * rb[k]
        for q in list(range(p + 1, 16)) + list(range(p)):
            t = rows[q]
            even = jnp.where(panel, 0.0, t)
            odd = None
            for j in range(8):
                m = lane_b(t, base + j) * rb[j]
                if j % 2 == 0:
                    even = even - m
                else:
                    odd = m if odd is None else odd + m
            rows[q] = even - odd
        out = rb[0]
        for i in range(1, 8):
            out = jnp.where(sub == i, rb[i], out)
        rows[p] = out
    return rows


def eliminate(o_ref, d_ref, y_ref, n):
    blocks = n // W

    def save(block):
        rows = invert_block([block[8 * q : 8 * q + 8, :] for q in range(16)])
        return jnp.concatenate(rows, axis=0)

    def step(kb, ahead):
        blk = pl.ds(pl.multiple_of(kb * W, W), W)
        dinv = d_ref[...]
        if ahead:
            nxt = pl.ds(pl.multiple_of(jnp.where(kb == blocks, 0, kb + 1) * W, W), W)
            following = save(o_ref[nxt, nxt] - dot(o_ref[nxt, blk], dot(dinv, o_ref[blk, nxt])))
        col = o_ref[:, blk]
        y_ref[...] = dot(dinv, o_ref[blk, :])
        y_ref[:, blk] = dinv
        o_ref[:, blk] = jnp.zeros((n + W, W), F32)
        o_ref[...] = o_ref[...] - dot(col, y_ref[...])
        o_ref[blk, :] = y_ref[...]
        if ahead:
            d_ref[...] = following

    def body(trip, carry):
        step(jnp.where(trip == 0, blocks, trip - 1), True)
        return carry

    d_ref[...] = jnp.zeros((W, W), F32)
    o_ref[n:, :] = jnp.zeros((W, n + W), F32)
    o_ref[:, n:] = jnp.zeros((n + W, W), F32)
    lax.fori_loop(0, blocks, body, 0)
    step(blocks - 1, False)


def put_rows(full_ref, at, pieces_ref, j):
    for g in range(full_ref.shape[0]):
        full_ref[g, at, :] = pieces_ref[j, :, W * g : W * g + W]


def flat(full_ref, rows):
    return jnp.concatenate([full_ref[g, rows, :] for g in range(full_ref.shape[0])], axis=1)


def pack_pairs(core, offs_ref, own_ref, other_ref, full_ref, cap):
    def body(j, carry):
        for k in range(2):
            at = pl.ds(offs_ref[2 * j + k], cap)

            @pl.when(core == k)
            def _():
                put_rows(full_ref, at, own_ref, j)

            @pl.when(core != k)
            def _():
                put_rows(full_ref, at, other_ref, j)

        return carry

    lax.fori_loop(0, 8, body, 0)


def inverse_kernel(
    offs_ref, core_ref, own_ref, other_ref, var_ref, o_ref, full_ref, s_ref, d_ref, y_ref, *, n, cap
):
    pack_pairs(core_ref[0], offs_ref, own_ref, other_ref, full_ref, cap)
    diag = lax.broadcasted_iota(jnp.int32, (W, W), 1) == lax.broadcasted_iota(jnp.int32, (W, W), 0)

    def body(g, carry):
        at = pl.ds(pl.multiple_of(W * g, W), W)
        s_ref[at, 0:n] = flat(full_ref, at)
        s_ref[at, at] = s_ref[at, at] + jnp.where(diag, var_ref[0:1, at], 0.0)
        return carry

    lax.fori_loop(0, n // W, body, 0)
    eliminate(s_ref, d_ref, y_ref, n)
    o_ref[...] = s_ref[0:n, 0:n]


VM = pl.BlockSpec(memory_space=pltpu.VMEM)
SM = pl.BlockSpec(memory_space=pltpu.SMEM)


def inverse(offs, core, own, other, variances):
    n = variances.shape[0]
    cap = own.shape[1]
    return pl.pallas_call(
        functools.partial(inverse_kernel, n=n, cap=cap),
        out_shape=jax.ShapeDtypeStruct((n, n), F32),
        in_specs=[SM, SM, VM, VM, VM],
        out_specs=VM,
        scratch_shapes=[
            pltpu.VMEM((n // W, n + cap, W), F32),
            pltpu.VMEM((n + W, n + W), F32),
            pltpu.VMEM((W, W), F32),
            pltpu.VMEM((W, n + W), F32),
        ],
        name="inverse",
    )(offs, core, own, other, jnp.broadcast_to(variances[None, :], (8, n)))


def select_kernel(ridx_ref, cidx_ref, cov_ref, x_ref, y_ref, c_ref):
    for i in range(x_ref.shape[0]):
        x_ref[i : i + 1, :] = cov_ref[pl.ds(ridx_ref[i], 1), :]
    lanes = lax.broadcasted_iota(jnp.int32, (y_ref.shape[0], cov_ref.shape[1]), 1)
    pick = jnp.where(lanes == cidx_ref[...], 1.0, 0.0)
    corner = dot(pick, x_ref[...], ((1,), (1,)))
    for k in range(c_ref.shape[0]):
        c_ref[k] = corner
    pick_columns(pick, cov_ref, y_ref)


def pick_columns(pick, mat_ref, o_ref):
    def body(g, carry):
        at = pl.ds(pl.multiple_of(2 * W * g, 2 * W), 2 * W)
        o_ref[:, at] = dot(pick, mat_ref[at, :], ((1,), (1,)))
        return carry

    lax.fori_loop(0, mat_ref.shape[0] // (2 * W), body, 0)


def pick_kernel(cidx_ref, mat_ref, o_ref):
    step = 96

    def body(g, carry):
        at = pl.ds(pl.multiple_of(step * g, 8), step)
        lanes = lax.broadcasted_iota(jnp.int32, (step, mat_ref.shape[1]), 1)
        pick = jnp.where(lanes == cidx_ref[at, :], 1.0, 0.0)
        pick_columns(pick, mat_ref, o_ref.at[at, :])
        return carry

    lax.fori_loop(0, o_ref.shape[0] // step, body, 0)


def picked(cidx, mat):
    return pl.pallas_call(
        pick_kernel,
        out_shape=jax.ShapeDtypeStruct((cidx.shape[0], mat.shape[0]), F32),
        in_specs=[VM, VM],
        out_specs=VM,
        name="picked",
    )(cidx[:, None], mat)


def select(ridx, cidx, cov):
    rows, cols = cov.shape
    return pl.pallas_call(
        select_kernel,
        out_shape=(
            jax.ShapeDtypeStruct((ridx.shape[0], cols), F32),
            jax.ShapeDtypeStruct((cidx.shape[0], rows), F32),
            jax.ShapeDtypeStruct((8, cidx.shape[0], ridx.shape[0]), F32),
        ),
        in_specs=[SM, VM, VM],
        out_specs=(VM, VM, VM),
        name="select",
    )(ridx, cidx[:, None], cov)


def widen_kernel(slot_ref, p_ref, o_ref):
    n = o_ref.shape[2]
    lanes = lax.broadcasted_iota(jnp.int32, (p_ref.shape[2], n), 1)

    def body(r, total):
        put = jnp.where(lanes == slot_ref[r], 1.0, 0.0)
        return total + dot(p_ref[r], put)

    total = lax.fori_loop(0, p_ref.shape[0], body, jnp.zeros((p_ref.shape[1], n), F32))
    for k in range(o_ref.shape[0]):
        o_ref[k] = total


def widen(slots, pieces, n):
    return pl.pallas_call(
        widen_kernel,
        out_shape=jax.ShapeDtypeStruct((8, pieces.shape[1], n), F32),
        in_specs=[VM, VM],
        out_specs=VM,
        name="widen",
    )(slots[:, :, None], pieces)


def final_kernel(
    roffs_ref, coffs_ref, row_ref, core_ref, inv_ref, x0, x1, x2, x3, own_ref, other_ref, prior_ref,
    o_ref, xs_ref, ys_ref, gain_ref,
):
    n = inv_ref.shape[0]
    pairs = (x0, x1, x2, x3)
    row = row_ref[0]

    def pack(b, carry):
        for k, pair in enumerate(pairs):

            @pl.when((row // 2 - b) % len(pairs) == k)
            def _():
                for h in range(2):
                    at = pl.ds(roffs_ref[2 * b + h], pair.shape[1])
                    put_rows(xs_ref, at, pair, (row - h) % 2)

        return carry

    lax.fori_loop(0, len(pairs), pack, 0)
    pack_pairs(core_ref[0], coffs_ref, own_ref, other_ref, ys_ref, own_ref.shape[1])
    gain_ref[...] = dot(inv_ref[...], flat(xs_ref, slice(0, n)))
    per = 2

    def body(g, carry):
        cells = jnp.concatenate([ys_ref[per * g + i, 0:n, :] for i in range(per)], axis=1)
        at = pl.ds(pl.multiple_of(per * W * g, W), per * W)
        o_ref[at, :] = prior_ref[at, :] - dot(cells, gain_ref[...], ((0,), (0,)))
        return carry

    lax.fori_loop(0, o_ref.shape[0] // (per * W), body, 0)


def final(roffs, coffs, row, core, inv, pairs, own, other, prior):
    n = inv.shape[0]
    return pl.pallas_call(
        final_kernel,
        out_shape=jax.ShapeDtypeStruct(prior.shape, F32),
        in_specs=[SM, SM, SM, SM] + [VM] * 8,
        out_specs=VM,
        scratch_shapes=[
            pltpu.VMEM((prior.shape[1] // W, n + pairs[0].shape[1], W), F32),
            pltpu.VMEM((prior.shape[0] // W, n + own.shape[1], W), F32),
            pltpu.VMEM((n, prior.shape[1]), F32),
        ],
        name="update",
    )(roffs, coffs, row, core, inv, *pairs, own, other, prior)


def stencil_table(wind, diffusivity):
    east_wind = wind[0]
    north_wind = wind[1]
    from_west = diffusivity + jnp.maximum(east_wind, 0.0)
    from_east = diffusivity + jnp.maximum(-east_wind, 0.0)
    from_north = diffusivity + jnp.maximum(north_wind, 0.0)
    from_south = diffusivity + jnp.maximum(-north_wind, 0.0)
    center = 1.0 - (from_west + from_east + from_north + from_south)
    x = lax.broadcasted_iota(jnp.int32, from_west.shape, 1)
    from_west = jnp.where(x > 0, from_west, 0.0)
    from_east = jnp.where(x < W - 1, from_east, 0.0)
    return jnp.stack([center, from_west, from_east, from_north, from_south])


def lane_pass(segs, w_ref, first):
    out = []
    for g in range(1, len(segs) - 1):
        at = slice(first + g, first + g + 1)
        v = segs[g]
        out.append(
            w_ref[0, at, :] * v
            + w_ref[1, at, :] * pltpu.roll(v, 1, 1)
            + w_ref[2, at, :] * pltpu.roll(v, W - 1, 1)
            + w_ref[3, at, :] * segs[g - 1]
            + w_ref[4, at, :] * segs[g + 1]
        )
    return out


def cols_kernel(w_ref, b_ref, low_ref, high_ref, o_ref, *, step):
    copies = o_ref.shape[0] if len(o_ref.shape) == 3 else 0

    def body(t, carry):
        at = pl.ds(pl.multiple_of(step * t, 8), step)
        segs = [low_ref[at, 0:W], low_ref[at, W : 2 * W]]
        segs += [b_ref[at, W * g : W * g + W] for g in range(b_ref.shape[1] // W)]
        segs += [high_ref[at, 0:W], high_ref[at, W : 2 * W]]
        segs = lane_pass(lane_pass(segs, w_ref, 0), w_ref, 1)
        for g, v in enumerate(segs):
            lanes = slice(W * g, W * g + W)
            if copies:
                for k in range(copies):
                    o_ref[k, at, lanes] = v
            else:
                o_ref[at, lanes] = v
        return carry

    lax.fori_loop(0, b_ref.shape[0] // step, body, 0)


def twice_cols(weights, block, low, high, copies=0):
    step = 24 if block.shape[0] % 64 else 64
    shape = ((copies,) if copies else ()) + block.shape
    return pl.pallas_call(
        functools.partial(cols_kernel, step=step),
        out_shape=jax.ShapeDtypeStruct(shape, F32),
        in_specs=[VM, VM, VM, VM],
        out_specs=VM,
        name="stencil_lanes",
    )(weights, block, low, high)


def rows_kernel(w_ref, b_ref, low_ref, high_ref, o_ref, mid_ref):
    n = b_ref.shape[0] // W
    cols = b_ref.shape[1]

    def coef(k, g):
        return jnp.broadcast_to(w_ref[g, :, k : k + 1], (W, cols))

    def one(v, north, south, g):
        return (
            coef(0, g) * v
            + coef(1, g) * pltpu.roll(v, 1, 0)
            + coef(2, g) * pltpu.roll(v, W - 1, 0)
            + coef(3, g) * north
            + coef(4, g) * south
        )

    def src(g):
        if g < 2:
            return low_ref[W * g : W * g + W, :]
        if g < n + 2:
            return b_ref[W * (g - 2) : W * (g - 2) + W, :]
        return high_ref[W * (g - n - 2) : W * (g - n - 2) + W, :]

    def first(g):
        mid_ref[pl.ds(pl.multiple_of(W * (g - 1), W), W), :] = one(
            src(g), src(g - 1), src(g + 1), g
        )

    def inner(g, carry):
        at = pl.multiple_of(W * (g - 2), W)
        v = b_ref[pl.ds(at, W), :]
        mid_ref[pl.ds(at + W, W), :] = one(v, b_ref[pl.ds(at - W, W), :], b_ref[pl.ds(at + W, W), :], g)
        return carry

    def second(g, carry):
        m = pl.multiple_of(W * (g - 1), W)
        o_ref[pl.ds(m - W, W), :] = one(
            mid_ref[pl.ds(m, W), :], mid_ref[pl.ds(m - W, W), :], mid_ref[pl.ds(m + W, W), :], g
        )
        return carry

    for g in (1, 2, n + 1, n + 2):
        first(g)
    lax.fori_loop(3, n + 1, inner, 0)
    lax.fori_loop(2, n + 2, second, 0)


def twice_rows(weights, block, low, high):
    return pl.pallas_call(
        rows_kernel,
        out_shape=jax.ShapeDtypeStruct(block.shape, F32),
        in_specs=[VM, VM, VM, VM],
        out_specs=VM,
        scratch_shapes=[pltpu.VMEM((block.shape[0] + 2 * W, block.shape[1]), F32)],
        name="stencil_rows",
    )(weights, block, low, high)


def prior_kernel(gap_ref, w_ref, wr_ref, noise_ref, b_ref, low_ref, high_ref, o_ref, mid_ref):
    nseg = b_ref.shape[1] // W
    lane = lax.broadcasted_iota(jnp.int32, (W, W), 1)
    sub = lax.broadcasted_iota(jnp.int32, (W, W), 0)
    step = 32

    def body(t, carry):
        base = pl.multiple_of(W * t, W)
        for h in range(W // step):
            at = pl.ds(base + step * h, step)
            segs = [low_ref[at, 0:W], low_ref[at, W : 2 * W]]
            segs += [b_ref[at, W * g : W * g + W] for g in range(nseg)]
            segs += [high_ref[at, 0:W], high_ref[at, W : 2 * W]]
            for g, v in enumerate(lane_pass(segs, w_ref, 0)):
                mid_ref[g, step * h : step * h + step, :] = v
        ahead = gap_ref[0] + 1 - t
        for g in range(nseg + 2):

            @pl.when(jnp.abs(ahead + g) <= 1)
            def _():
                here = W * (ahead + g) + lane - sub
                coef = [jnp.broadcast_to(wr_ref[t + 2, :, k : k + 1], (W, W)) for k in range(5)]
                spread = jnp.where(here == 0, coef[0], 0.0)
                spread = jnp.where(here == -1, coef[1], spread)
                spread = jnp.where(here == 1, coef[2], spread)
                spread = jnp.where(here == -W, coef[3], spread)
                spread = jnp.where(here == W, coef[4], spread)
                mid_ref[g] = mid_ref[g] + spread * noise_ref[g + 1 : g + 2, :]

        for h in range(W // step):
            at = pl.ds(base + step * h, step)
            mid = [mid_ref[g, step * h : step * h + step, :] for g in range(nseg + 2)]
            for g, v in enumerate(lane_pass(mid, w_ref, 1)):
                o_ref[at, W * g : W * g + W] = v
        for g in range(nseg):

            @pl.when(ahead + g + 1 == 0)
            def _():
                at = pl.ds(base, W)
                lanes = slice(W * g, W * g + W)
                last = jnp.where(lane == sub, noise_ref[g + 2 : g + 3, :], 0.0)
                o_ref[at, lanes] = o_ref[at, lanes] + last

        return carry

    lax.fori_loop(0, o_ref.shape[0] // W, body, 0)


def prior_cols(gap, weights, row_weights, noise, block, low, high):
    return pl.pallas_call(
        prior_kernel,
        out_shape=jax.ShapeDtypeStruct(block.shape, F32),
        in_specs=[SM, VM, VM, VM, VM, VM, VM],
        out_specs=VM,
        scratch_shapes=[pltpu.VMEM((block.shape[1] // W + 2, W, W), F32)],
        name="prior_lanes",
    )(gap, weights, row_weights, noise, block, low, high)


def halos(block, axis, dim, width):
    count = lax.axis_size(axis)
    forward = [(i, i + 1) for i in range(count - 1)]
    backward = [(target, source) for source, target in forward]
    low = lax.ppermute(
        lax.slice_in_dim(block, block.shape[dim] - width, None, axis=dim), axis, forward
    )
    high = lax.ppermute(lax.slice_in_dim(block, 0, width, axis=dim), axis, backward)
    return low, high


def gather_sum(parts, axis):
    count = lax.axis_size(axis)
    size = parts.shape[0] // count
    pieces = lax.all_to_all(parts.reshape(count, size, -1), axis, 0, 0)
    mine = jnp.sum(pieces, axis=0)
    full = lax.all_to_all(jnp.broadcast_to(mine[None], (count,) + mine.shape), axis, 0, 0)
    return full.reshape(parts.shape)


def share(copies, axis, groups=None):
    return lax.all_to_all(copies, axis, 0, 0, axis_index_groups=groups)


def windows(array, cap, count):
    size = array.shape[0] // count
    padded = jnp.pad(array, ((0, cap), (0, 0)))
    return jnp.stack([padded[size * i : size * i + cap] for i in range(count)])


def local(cov, obs_cells, obs_var, wind, diffusivity, noise):
    rows_here, cols_here = cov.shape
    row = lax.axis_index("row")
    col = lax.axis_index("col")
    row_start = row * rows_here
    col_start = col * cols_here
    core = (col % 2)[None]
    same_core = [[c for c in range(COLS) if c % 2 == k] for k in range(2)]
    swap = [(c, c ^ 1) for c in range(COLS)]

    cells = obs_cells.reshape(-1)
    n = cells.shape[0]
    ids = jnp.arange(n, dtype=jnp.int32)
    key = (cells // cols_here) * n + ids
    place = jnp.sum((key[None, :] < key[:, None]).astype(jnp.int32), axis=1)
    at = place[:, None] == ids[None, :]
    ordered = jnp.sum(jnp.where(at, cells[:, None], 0), axis=0)
    variances = jnp.sum(jnp.where(at, obs_var.reshape(-1)[:, None], 0.0), axis=0)
    edges = jnp.arange(COLS + 1, dtype=jnp.int32) * cols_here
    bounds = jnp.sum((cells[None, :] < edges[:, None]).astype(jnp.int32), axis=1)
    col_offs = bounds[:-1]
    row_bounds = bounds[:: COLS // ROWS]
    row_offs = row_bounds[:-1]
    row_counts = row_bounds[1:] - row_bounds[:-1]
    fits = (jnp.max(row_counts) <= CAP_ROW) & (jnp.max(bounds[1:] - bounds[:-1]) <= CAP_COL)

    padded = jnp.pad(ordered, (0, CAP_ROW))
    ridx = lax.dynamic_slice_in_dim(padded, row_offs[row], CAP_ROW) - row_start
    cidx = lax.dynamic_slice_in_dim(padded, col_offs[col], CAP_COL) - col_start
    ridx = jnp.clip(ridx, 0, rows_here - 1)
    cidx = jnp.clip(cidx, 0, cols_here - 1)
    lanes = jnp.arange(CAP_ROW, dtype=jnp.int32)[None, :]
    slots = jnp.where(lanes < row_counts[:, None], row_offs[:, None] + lanes, -1)

    margin = 2 * W
    grid_row = row_start // W
    grid_col = col_start // W
    table = jnp.pad(stencil_table(wind, diffusivity), ((0, 0), (2, 2), (0, 0)))
    row_w = lax.dynamic_slice_in_dim(table, grid_row, rows_here // W + 4, 1)
    col_w = lax.dynamic_slice_in_dim(table, grid_col, cols_here // W + 4, 1)
    noise_cols = lax.dynamic_slice_in_dim(
        jnp.pad(noise, ((2, 2), (0, 0))), grid_col, cols_here // W + 4, 0
    )
    row_sub = jnp.transpose(row_w, (1, 2, 0))

    xg, yg, cg = select(ridx, cidx, cov)
    c_pieces = share(cg, "row")
    row_halo = halos(cov, "row", 0, margin)
    y_halo = halos(yg, "row", 1, margin)
    c_rows = widen(slots, c_pieces, n)
    c_own = share(c_rows, "col", same_core)
    c_other = lax.ppermute(c_own, "col", swap)

    tall = twice_rows(row_sub, cov, *row_halo)
    col_halo = halos(tall, "col", 1, margin)
    gap = (grid_col - 2 - grid_row)[None]
    prior = prior_cols(gap, col_w, row_sub, noise_cols, tall, *col_halo)

    x_halo = halos(xg, "col", 1, margin)
    vx = twice_cols(col_w, xg, *x_halo)
    vy = twice_cols(row_w, yg, *y_halo, copies=8)
    pair = jnp.stack([vx, lax.ppermute(vx, "row", [(i, i ^ 1) for i in range(ROWS)])])
    pairs = (pair,) + tuple(
        lax.ppermute(pair, "row", [(i, (i + 2 * k) % ROWS) for i in range(ROWS)])
        for k in range(1, ROWS // 2)
    )
    y_own = share(vy, "col", same_core)
    y_other = lax.ppermute(y_own, "col", swap)

    blocks = jnp.arange(ROWS, dtype=jnp.int32)

    def long_x():
        hit = (ordered >= row_start) & (ordered < row_start + rows_here)
        part = cov[jnp.clip(ordered - row_start, 0, rows_here - 1), :]
        return gather_sum(jnp.where(hit[:, None], part, 0.0), "row")

    def cores(array):
        parts = windows(array, CAP_COL, COLS)
        parts = parts.reshape((COLS // 2, 2) + parts.shape[1:])
        return tuple(
            lax.dynamic_index_in_dim(parts, k, 1, keepdims=False) for k in (core[0], 1 - core[0])
        )

    even_cols = jnp.arange(COLS, dtype=jnp.int32) * (n // COLS)
    even_rows = blocks * (n // ROWS)

    def long_corner():
        own, other = cores(gather_sum(picked(ordered - col_start, long_x()), "col"))
        return even_cols, own, other

    def long_update():
        x = long_x()
        y = gather_sum(picked(ordered - col_start, cov), "col")
        x = twice_cols(col_w, x, *halos(x, "col", 1, margin))
        y = twice_cols(row_w, y, *halos(y, "row", 1, margin))
        pieces = windows(x, CAP_ROW, ROWS).reshape((ROWS // 2, 2, CAP_ROW, -1))
        pieces = jnp.stack(
            [lax.dynamic_index_in_dim(pieces, (row + k) % 2, 1, keepdims=False) for k in range(2)], 1
        )
        sets = tuple(
            lax.dynamic_index_in_dim(pieces, (row // 2 - k) % (ROWS // 2), 0, keepdims=False)
            for k in range(ROWS // 2)
        )
        return (even_rows, even_cols, sets) + cores(y)

    def unless(fits, short, long):
        def body(state):
            return jnp.bool_(False), long()

        return lax.while_loop(lambda state: state[0], body, (~fits, short))[1]

    c_offs, c_own, c_other = unless(fits, (col_offs, c_own, c_other), long_corner)
    inv = inverse(c_offs, core, c_own, c_other, variances)
    x_offs, y_offs, pairs, y_own, y_other = unless(
        fits, (row_offs, col_offs, pairs, y_own, y_other), long_update
    )
    return final(x_offs, y_offs, row[None], core, inv, pairs, y_own, y_other, prior)


def solution(mesh):
    placed = (P("row", "col"), P(), P(), P(), P(), P())

    return jax.shard_map(
        local, mesh=mesh, in_specs=placed, out_specs=P("row", "col"), check_vma=False
    )
```

```python
import functools

import jax
import jax.numpy as jnp
from jax import lax
from jax.experimental import pallas as pl
from jax.experimental.pallas import tpu as pltpu
from jax.sharding import PartitionSpec as P


HI = lax.Precision.HIGHEST
F32 = jnp.float32
W = 128
ROWS = 8
COLS = 16
CAP_ROW = 128
CAP_COL = 72


def dot(a, b, dims=((1,), (0,)), precision=HI):
    return lax.dot_general(a, b, (dims, ((), ())), precision=precision, preferred_element_type=F32)


def recip(x):
    r = pltpu.reciprocal(x, approx=True)
    return r * (2.0 - x * r)


def lane_b(v, lane):
    return jnp.broadcast_to(v[:, lane : lane + 1], (8, 128))


def sub_b(v, sub):
    return jnp.broadcast_to(v[sub : sub + 1, :], (8, 128))


def invert_block(rows):
    lane = lax.broadcasted_iota(jnp.int32, (8, 128), 1)
    sub = lax.broadcasted_iota(jnp.int32, (8, 128), 0)
    rows = list(rows)
    for p in range(16):
        base = 8 * p
        panel = (lane >= base) & (lane < base + 8)
        src = rows[p]
        rb = [sub_b(src, i) for i in range(8)]
        e = [[lane_b(rb[i], base + j) if j >= i else None for j in range(8)] for i in range(8)]
        rb = [jnp.where(panel, jnp.where(lane == base + i, 1.0, 0.0), rb[i]) for i in range(8)]
        for k in range(8):
            r = recip(e[k][k])
            f = [e[i][k] if i < k else e[k][i] for i in range(8)]
            for j in range(k + 1, 8):
                e[k][j] = e[k][j] * r
            rb[k] = rb[k] * r
            for i in range(8):
                if i == k:
                    continue
                for j in range(max(i, k + 1), 8):
                    e[i][j] = e[i][j] - f[i] * e[k][j]
                rb[i] = rb[i] - f[i] * rb[k]
        for q in list(range(p + 1, 16)) + list(range(p)):
            t = rows[q]
            even = jnp.where(panel, 0.0, t)
            odd = None
            for j in range(8):
                m = lane_b(t, base + j) * rb[j]
                if j % 2 == 0:
                    even = even - m
                else:
                    odd = m if odd is None else odd + m
            rows[q] = even - odd
        out = rb[0]
        for i in range(1, 8):
            out = jnp.where(sub == i, rb[i], out)
        rows[p] = out
    return rows


def eliminate(o_ref, d_ref, y_ref, n):
    blocks = n // W

    def save(block):
        rows = invert_block([block[8 * q : 8 * q + 8, :] for q in range(16)])
        return jnp.concatenate(rows, axis=0)

    def step(kb, ahead):
        blk = pl.ds(pl.multiple_of(kb * W, W), W)
        dinv = d_ref[...]
        if ahead:
            nxt = pl.ds(pl.multiple_of(jnp.where(kb == blocks, 0, kb + 1) * W, W), W)
            following = save(o_ref[nxt, nxt] - dot(o_ref[nxt, blk], dot(dinv, o_ref[blk, nxt])))
        col = o_ref[:, blk]
        y_ref[...] = dot(dinv, o_ref[blk, :])
        y_ref[:, blk] = dinv
        o_ref[:, blk] = jnp.zeros((n + W, W), F32)
        o_ref[...] = o_ref[...] - dot(col, y_ref[...])
        o_ref[blk, :] = y_ref[...]
        if ahead:
            d_ref[...] = following

    def body(trip, carry):
        step(jnp.where(trip == 0, blocks, trip - 1), True)
        return carry

    d_ref[...] = jnp.zeros((W, W), F32)
    o_ref[n:, :] = jnp.zeros((W, n + W), F32)
    o_ref[:, n:] = jnp.zeros((n + W, W), F32)
    lax.fori_loop(0, blocks, body, 0)
    step(blocks - 1, False)


def put_rows(full_ref, at, pieces_ref, j):
    for g in range(full_ref.shape[0]):
        full_ref[g, at, :] = pieces_ref[j, :, W * g : W * g + W]


def flat(full_ref, rows):
    return jnp.concatenate([full_ref[g, rows, :] for g in range(full_ref.shape[0])], axis=1)


def pack_pairs(core, offs_ref, own_ref, other_ref, full_ref, cap):
    def body(j, carry):
        for k in range(2):
            at = pl.ds(offs_ref[2 * j + k], cap)

            @pl.when(core == k)
            def _():
                put_rows(full_ref, at, own_ref, j)

            @pl.when(core != k)
            def _():
                put_rows(full_ref, at, other_ref, j)

        return carry

    lax.fori_loop(0, 8, body, 0)


def inverse_kernel(
    offs_ref, core_ref, own_ref, other_ref, var_ref, o_ref, full_ref, s_ref, d_ref, y_ref, *, n, cap
):
    pack_pairs(core_ref[0], offs_ref, own_ref, other_ref, full_ref, cap)
    diag = lax.broadcasted_iota(jnp.int32, (W, W), 1) == lax.broadcasted_iota(jnp.int32, (W, W), 0)

    def body(g, carry):
        at = pl.ds(pl.multiple_of(W * g, W), W)
        s_ref[at, 0:n] = flat(full_ref, at)
        s_ref[at, at] = s_ref[at, at] + jnp.where(diag, var_ref[0:1, at], 0.0)
        return carry

    lax.fori_loop(0, n // W, body, 0)
    eliminate(s_ref, d_ref, y_ref, n)
    o_ref[...] = s_ref[0:n, 0:n]


VM = pl.BlockSpec(memory_space=pltpu.VMEM)
SM = pl.BlockSpec(memory_space=pltpu.SMEM)


def inverse(offs, core, own, other, variances):
    n = variances.shape[0]
    cap = own.shape[1]
    return pl.pallas_call(
        functools.partial(inverse_kernel, n=n, cap=cap),
        out_shape=jax.ShapeDtypeStruct((n, n), F32),
        in_specs=[SM, SM, VM, VM, VM],
        out_specs=VM,
        scratch_shapes=[
            pltpu.VMEM((n // W, n + cap, W), F32),
            pltpu.VMEM((n + W, n + W), F32),
            pltpu.VMEM((W, W), F32),
            pltpu.VMEM((W, n + W), F32),
        ],
        name="inverse",
    )(offs, core, own, other, jnp.broadcast_to(variances[None, :], (8, n)))


def select_kernel(ridx_ref, cidx_ref, cov_ref, x_ref, y_ref, c_ref):
    for i in range(x_ref.shape[0]):
        x_ref[i : i + 1, :] = cov_ref[pl.ds(ridx_ref[i], 1), :]
    lanes = lax.broadcasted_iota(jnp.int32, (y_ref.shape[0], cov_ref.shape[1]), 1)
    pick = jnp.where(lanes == cidx_ref[...], 1.0, 0.0)
    corner = dot(pick, x_ref[...], ((1,), (1,)))
    for k in range(c_ref.shape[0]):
        c_ref[k] = corner
    pick_columns(pick, cov_ref, y_ref)


def pick_columns(pick, mat_ref, o_ref):
    def body(g, carry):
        at = pl.ds(pl.multiple_of(2 * W * g, 2 * W), 2 * W)
        o_ref[:, at] = dot(pick, mat_ref[at, :], ((1,), (1,)))
        return carry

    lax.fori_loop(0, mat_ref.shape[0] // (2 * W), body, 0)


def pick_kernel(cidx_ref, mat_ref, o_ref):
    step = 96

    def body(g, carry):
        at = pl.ds(pl.multiple_of(step * g, 8), step)
        lanes = lax.broadcasted_iota(jnp.int32, (step, mat_ref.shape[1]), 1)
        pick = jnp.where(lanes == cidx_ref[at, :], 1.0, 0.0)
        pick_columns(pick, mat_ref, o_ref.at[at, :])
        return carry

    lax.fori_loop(0, o_ref.shape[0] // step, body, 0)


def picked(cidx, mat):
    return pl.pallas_call(
        pick_kernel,
        out_shape=jax.ShapeDtypeStruct((cidx.shape[0], mat.shape[0]), F32),
        in_specs=[VM, VM],
        out_specs=VM,
        name="picked",
    )(cidx[:, None], mat)


def select(ridx, cidx, cov):
    rows, cols = cov.shape
    return pl.pallas_call(
        select_kernel,
        out_shape=(
            jax.ShapeDtypeStruct((ridx.shape[0], cols), F32),
            jax.ShapeDtypeStruct((cidx.shape[0], rows), F32),
            jax.ShapeDtypeStruct((8, cidx.shape[0], ridx.shape[0]), F32),
        ),
        in_specs=[SM, VM, VM],
        out_specs=(VM, VM, VM),
        name="select",
    )(ridx, cidx[:, None], cov)


def widen_kernel(slot_ref, p_ref, o_ref):
    n = o_ref.shape[2]
    lanes = lax.broadcasted_iota(jnp.int32, (p_ref.shape[2], n), 1)

    def body(r, total):
        put = jnp.where(lanes == slot_ref[r], 1.0, 0.0)
        return total + dot(p_ref[r], put)

    total = lax.fori_loop(0, p_ref.shape[0], body, jnp.zeros((p_ref.shape[1], n), F32))
    for k in range(o_ref.shape[0]):
        o_ref[k] = total


def widen(slots, pieces, n):
    return pl.pallas_call(
        widen_kernel,
        out_shape=jax.ShapeDtypeStruct((8, pieces.shape[1], n), F32),
        in_specs=[VM, VM],
        out_specs=VM,
        name="widen",
    )(slots[:, :, None], pieces)


def gain_kernel(offs_ref, row_ref, inv_ref, x0, x1, x2, x3, o_ref, xs_ref):
    n = inv_ref.shape[0]
    pairs = (x0, x1, x2, x3)
    row = row_ref[0]

    def pack(b, carry):
        for k, pair in enumerate(pairs):

            @pl.when((row // 2 - b) % len(pairs) == k)
            def _():
                for h in range(2):
                    at = pl.ds(offs_ref[2 * b + h], pair.shape[1])
                    put_rows(xs_ref, at, pair, (row - h) % 2)

        return carry

    lax.fori_loop(0, len(pairs), pack, 0)
    o_ref[...] = dot(inv_ref[...], flat(xs_ref, slice(0, n)))


def gained(offs, row, inv, pairs):
    n = inv.shape[0]
    cap, cols = pairs[0].shape[1:]
    return pl.pallas_call(
        gain_kernel,
        out_shape=jax.ShapeDtypeStruct((n, cols), F32),
        in_specs=[SM, SM] + [VM] * 5,
        out_specs=VM,
        scratch_shapes=[pltpu.VMEM((cols // W, n + cap, W), F32)],
        name="gain",
    )(offs, row, inv, *pairs)


def final_kernel(offs_ref, core_ref, gain_ref, own_ref, other_ref, prior_ref, o_ref, ys_ref):
    n = gain_ref.shape[0]
    pack_pairs(core_ref[0], offs_ref, own_ref, other_ref, ys_ref, own_ref.shape[1])
    per = 2

    def body(g, carry):
        cells = jnp.concatenate([ys_ref[per * g + i, 0:n, :] for i in range(per)], axis=1)
        at = pl.ds(pl.multiple_of(per * W * g, W), per * W)
        o_ref[at, :] = prior_ref[at, :] - dot(cells, gain_ref[...], ((0,), (0,)))
        return carry

    lax.fori_loop(0, o_ref.shape[0] // (per * W), body, 0)


def final(offs, core, gain, own, other, prior):
    return pl.pallas_call(
        final_kernel,
        out_shape=jax.ShapeDtypeStruct(prior.shape, F32),
        in_specs=[SM, SM] + [VM] * 4,
        out_specs=VM,
        scratch_shapes=[
            pltpu.VMEM((prior.shape[0] // W, gain.shape[0] + own.shape[1], W), F32),
        ],
        name="update",
    )(offs, core, gain, own, other, prior)


def stencil_table(wind, diffusivity):
    east_wind = wind[0]
    north_wind = wind[1]
    from_west = diffusivity + jnp.maximum(east_wind, 0.0)
    from_east = diffusivity + jnp.maximum(-east_wind, 0.0)
    from_north = diffusivity + jnp.maximum(north_wind, 0.0)
    from_south = diffusivity + jnp.maximum(-north_wind, 0.0)
    center = 1.0 - (from_west + from_east + from_north + from_south)
    x = lax.broadcasted_iota(jnp.int32, from_west.shape, 1)
    from_west = jnp.where(x > 0, from_west, 0.0)
    from_east = jnp.where(x < W - 1, from_east, 0.0)
    return jnp.stack([center, from_west, from_east, from_north, from_south])


def lane_pass(segs, w_ref, first):
    out = []
    for g in range(1, len(segs) - 1):
        at = slice(first + g, first + g + 1)
        v = segs[g]
        out.append(
            w_ref[0, at, :] * v
            + w_ref[1, at, :] * pltpu.roll(v, 1, 1)
            + w_ref[2, at, :] * pltpu.roll(v, W - 1, 1)
            + w_ref[3, at, :] * segs[g - 1]
            + w_ref[4, at, :] * segs[g + 1]
        )
    return out


def cols_kernel(w_ref, b_ref, low_ref, high_ref, o_ref, *, step):
    copies = o_ref.shape[0] if len(o_ref.shape) == 3 else 0

    def body(t, carry):
        at = pl.ds(pl.multiple_of(step * t, 8), step)
        segs = [low_ref[at, 0:W], low_ref[at, W : 2 * W]]
        segs += [b_ref[at, W * g : W * g + W] for g in range(b_ref.shape[1] // W)]
        segs += [high_ref[at, 0:W], high_ref[at, W : 2 * W]]
        segs = lane_pass(lane_pass(segs, w_ref, 0), w_ref, 1)
        for g, v in enumerate(segs):
            lanes = slice(W * g, W * g + W)
            if copies:
                for k in range(copies):
                    o_ref[k, at, lanes] = v
            else:
                o_ref[at, lanes] = v
        return carry

    lax.fori_loop(0, b_ref.shape[0] // step, body, 0)


def twice_cols(weights, block, low, high, copies=0):
    step = 24 if block.shape[0] % 64 else 64
    shape = ((copies,) if copies else ()) + block.shape
    return pl.pallas_call(
        functools.partial(cols_kernel, step=step),
        out_shape=jax.ShapeDtypeStruct(shape, F32),
        in_specs=[VM, VM, VM, VM],
        out_specs=VM,
        name="stencil_lanes",
    )(weights, block, low, high)


def rows_kernel(w_ref, b_ref, low_ref, high_ref, o_ref, mid_ref):
    n = b_ref.shape[0] // W
    cols = b_ref.shape[1]

    def coef(k, g):
        return jnp.broadcast_to(w_ref[g, :, k : k + 1], (W, cols))

    def one(v, north, south, g):
        return (
            coef(0, g) * v
            + coef(1, g) * pltpu.roll(v, 1, 0)
            + coef(2, g) * pltpu.roll(v, W - 1, 0)
            + coef(3, g) * north
            + coef(4, g) * south
        )

    def src(g):
        if g < 2:
            return low_ref[W * g : W * g + W, :]
        if g < n + 2:
            return b_ref[W * (g - 2) : W * (g - 2) + W, :]
        return high_ref[W * (g - n - 2) : W * (g - n - 2) + W, :]

    def first(g):
        mid_ref[pl.ds(pl.multiple_of(W * (g - 1), W), W), :] = one(
            src(g), src(g - 1), src(g + 1), g
        )

    def inner(g, carry):
        at = pl.multiple_of(W * (g - 2), W)
        v = b_ref[pl.ds(at, W), :]
        mid_ref[pl.ds(at + W, W), :] = one(v, b_ref[pl.ds(at - W, W), :], b_ref[pl.ds(at + W, W), :], g)
        return carry

    def second(g, carry):
        m = pl.multiple_of(W * (g - 1), W)
        o_ref[pl.ds(m - W, W), :] = one(
            mid_ref[pl.ds(m, W), :], mid_ref[pl.ds(m - W, W), :], mid_ref[pl.ds(m + W, W), :], g
        )
        return carry

    for g in (1, 2, n + 1, n + 2):
        first(g)
    lax.fori_loop(3, n + 1, inner, 0)
    lax.fori_loop(2, n + 2, second, 0)


def twice_rows(weights, block, low, high):
    return pl.pallas_call(
        rows_kernel,
        out_shape=jax.ShapeDtypeStruct(block.shape, F32),
        in_specs=[VM, VM, VM, VM],
        out_specs=VM,
        scratch_shapes=[pltpu.VMEM((block.shape[0] + 2 * W, block.shape[1]), F32)],
        name="stencil_rows",
    )(weights, block, low, high)


def prior_kernel(gap_ref, w_ref, wr_ref, noise_ref, b_ref, low_ref, high_ref, o_ref, mid_ref):
    nseg = b_ref.shape[1] // W
    lane = lax.broadcasted_iota(jnp.int32, (W, W), 1)
    sub = lax.broadcasted_iota(jnp.int32, (W, W), 0)
    step = 32

    def body(t, carry):
        base = pl.multiple_of(W * t, W)
        for h in range(W // step):
            at = pl.ds(base + step * h, step)
            segs = [low_ref[at, 0:W], low_ref[at, W : 2 * W]]
            segs += [b_ref[at, W * g : W * g + W] for g in range(nseg)]
            segs += [high_ref[at, 0:W], high_ref[at, W : 2 * W]]
            for g, v in enumerate(lane_pass(segs, w_ref, 0)):
                mid_ref[g, step * h : step * h + step, :] = v
        ahead = gap_ref[0] + 1 - t
        for g in range(nseg + 2):

            @pl.when(jnp.abs(ahead + g) <= 1)
            def _():
                here = W * (ahead + g) + lane - sub
                coef = [jnp.broadcast_to(wr_ref[t + 2, :, k : k + 1], (W, W)) for k in range(5)]
                spread = jnp.where(here == 0, coef[0], 0.0)
                spread = jnp.where(here == -1, coef[1], spread)
                spread = jnp.where(here == 1, coef[2], spread)
                spread = jnp.where(here == -W, coef[3], spread)
                spread = jnp.where(here == W, coef[4], spread)
                mid_ref[g] = mid_ref[g] + spread * noise_ref[g + 1 : g + 2, :]

        for h in range(W // step):
            at = pl.ds(base + step * h, step)
            mid = [mid_ref[g, step * h : step * h + step, :] for g in range(nseg + 2)]
            for g, v in enumerate(lane_pass(mid, w_ref, 1)):
                o_ref[at, W * g : W * g + W] = v
        for g in range(nseg):

            @pl.when(ahead + g + 1 == 0)
            def _():
                at = pl.ds(base, W)
                lanes = slice(W * g, W * g + W)
                last = jnp.where(lane == sub, noise_ref[g + 2 : g + 3, :], 0.0)
                o_ref[at, lanes] = o_ref[at, lanes] + last

        return carry

    lax.fori_loop(0, o_ref.shape[0] // W, body, 0)


def prior_cols(gap, weights, row_weights, noise, block, low, high):
    return pl.pallas_call(
        prior_kernel,
        out_shape=jax.ShapeDtypeStruct(block.shape, F32),
        in_specs=[SM, VM, VM, VM, VM, VM, VM],
        out_specs=VM,
        scratch_shapes=[pltpu.VMEM((block.shape[1] // W + 2, W, W), F32)],
        name="prior_lanes",
    )(gap, weights, row_weights, noise, block, low, high)


def halos(block, axis, dim, width):
    count = lax.axis_size(axis)
    forward = [(i, i + 1) for i in range(count - 1)]
    backward = [(target, source) for source, target in forward]
    low = lax.ppermute(
        lax.slice_in_dim(block, block.shape[dim] - width, None, axis=dim), axis, forward
    )
    high = lax.ppermute(lax.slice_in_dim(block, 0, width, axis=dim), axis, backward)
    return low, high


def gather_sum(parts, axis):
    count = lax.axis_size(axis)
    size = parts.shape[0] // count
    pieces = lax.all_to_all(parts.reshape(count, size, -1), axis, 0, 0)
    mine = jnp.sum(pieces, axis=0)
    full = lax.all_to_all(jnp.broadcast_to(mine[None], (count,) + mine.shape), axis, 0, 0)
    return full.reshape(parts.shape)


def share(copies, axis, groups=None):
    return lax.all_to_all(copies, axis, 0, 0, axis_index_groups=groups)


def windows(array, cap, count):
    size = array.shape[0] // count
    padded = jnp.pad(array, ((0, cap), (0, 0)))
    return jnp.stack([padded[size * i : size * i + cap] for i in range(count)])


def local(cov, obs_cells, obs_var, wind, diffusivity, noise):
    rows_here, cols_here = cov.shape
    row = lax.axis_index("row")
    col = lax.axis_index("col")
    row_start = row * rows_here
    col_start = col * cols_here
    core = (col % 2)[None]
    same_core = [[c for c in range(COLS) if c % 2 == k] for k in range(2)]
    swap = [(c, c ^ 1) for c in range(COLS)]

    cells = obs_cells.reshape(-1)
    n = cells.shape[0]
    ids = jnp.arange(n, dtype=jnp.int32)
    key = (cells // cols_here) * n + ids
    place = jnp.sum((key[None, :] < key[:, None]).astype(jnp.int32), axis=1)
    at = place[:, None] == ids[None, :]
    ordered = jnp.sum(jnp.where(at, cells[:, None], 0), axis=0)
    variances = jnp.sum(jnp.where(at, obs_var.reshape(-1)[:, None], 0.0), axis=0)
    edges = jnp.arange(COLS + 1, dtype=jnp.int32) * cols_here
    bounds = jnp.sum((cells[None, :] < edges[:, None]).astype(jnp.int32), axis=1)
    col_offs = bounds[:-1]
    row_bounds = bounds[:: COLS // ROWS]
    row_offs = row_bounds[:-1]
    row_counts = row_bounds[1:] - row_bounds[:-1]
    fits = (jnp.max(row_counts) <= CAP_ROW) & (jnp.max(bounds[1:] - bounds[:-1]) <= CAP_COL)

    padded = jnp.pad(ordered, (0, CAP_ROW))
    ridx = lax.dynamic_slice_in_dim(padded, row_offs[row], CAP_ROW) - row_start
    cidx = lax.dynamic_slice_in_dim(padded, col_offs[col], CAP_COL) - col_start
    ridx = jnp.clip(ridx, 0, rows_here - 1)
    cidx = jnp.clip(cidx, 0, cols_here - 1)
    lanes = jnp.arange(CAP_ROW, dtype=jnp.int32)[None, :]
    slots = jnp.where(lanes < row_counts[:, None], row_offs[:, None] + lanes, -1)

    margin = 2 * W
    grid_row = row_start // W
    grid_col = col_start // W
    table = jnp.pad(stencil_table(wind, diffusivity), ((0, 0), (2, 2), (0, 0)))
    row_w = lax.dynamic_slice_in_dim(table, grid_row, rows_here // W + 4, 1)
    col_w = lax.dynamic_slice_in_dim(table, grid_col, cols_here // W + 4, 1)
    noise_cols = lax.dynamic_slice_in_dim(
        jnp.pad(noise, ((2, 2), (0, 0))), grid_col, cols_here // W + 4, 0
    )
    row_sub = jnp.transpose(row_w, (1, 2, 0))

    xg, yg, cg = select(ridx, cidx, cov)
    c_pieces = share(cg, "row")
    row_halo = halos(cov, "row", 0, margin)
    y_halo = halos(yg, "row", 1, margin)
    c_rows = widen(slots, c_pieces, n)
    c_own = share(c_rows, "col", same_core)
    c_other = lax.ppermute(c_own, "col", swap)

    tall = twice_rows(row_sub, cov, *row_halo)
    col_halo = halos(tall, "col", 1, margin)
    gap = (grid_col - 2 - grid_row)[None]
    prior = prior_cols(gap, col_w, row_sub, noise_cols, tall, *col_halo)

    x_halo = halos(xg, "col", 1, margin)
    vx = twice_cols(col_w, xg, *x_halo)
    vy = twice_cols(row_w, yg, *y_halo, copies=8)
    pair = jnp.stack([vx, lax.ppermute(vx, "row", [(i, i ^ 1) for i in range(ROWS)])])
    pairs = (pair,) + tuple(
        lax.ppermute(pair, "row", [(i, (i + 2 * k) % ROWS) for i in range(ROWS)])
        for k in range(1, ROWS // 2)
    )
    y_own = share(vy, "col", same_core)
    y_other = lax.ppermute(y_own, "col", swap)

    blocks = jnp.arange(ROWS, dtype=jnp.int32)

    def long_x():
        hit = (ordered >= row_start) & (ordered < row_start + rows_here)
        part = cov[jnp.clip(ordered - row_start, 0, rows_here - 1), :]
        return gather_sum(jnp.where(hit[:, None], part, 0.0), "row")

    def cores(array):
        parts = windows(array, CAP_COL, COLS)
        parts = parts.reshape((COLS // 2, 2) + parts.shape[1:])
        return tuple(
            lax.dynamic_index_in_dim(parts, k, 1, keepdims=False) for k in (core[0], 1 - core[0])
        )

    even_cols = jnp.arange(COLS, dtype=jnp.int32) * (n // COLS)
    even_rows = blocks * (n // ROWS)

    def long_corner():
        own, other = cores(gather_sum(picked(ordered - col_start, long_x()), "col"))
        return even_cols, own, other

    def long_rows():
        x = long_x()
        x = twice_cols(col_w, x, *halos(x, "col", 1, margin))
        pieces = windows(x, CAP_ROW, ROWS).reshape((ROWS // 2, 2, CAP_ROW, -1))
        pieces = jnp.stack(
            [lax.dynamic_index_in_dim(pieces, (row + k) % 2, 1, keepdims=False) for k in range(2)], 1
        )
        sets = tuple(
            lax.dynamic_index_in_dim(pieces, (row // 2 - k) % (ROWS // 2), 0, keepdims=False)
            for k in range(ROWS // 2)
        )
        return even_rows, sets

    def long_cols():
        y = gather_sum(picked(ordered - col_start, cov), "col")
        return (even_cols,) + cores(twice_cols(row_w, y, *halos(y, "row", 1, margin)))

    def unless(fits, short, long):
        def body(state):
            return jnp.bool_(False), long()

        return lax.while_loop(lambda state: state[0], body, (~fits, short))[1]

    c_offs, c_own, c_other = unless(fits, (col_offs, c_own, c_other), long_corner)
    inv = inverse(c_offs, core, c_own, c_other, variances)
    x_offs, pairs = unless(fits, (row_offs, pairs), long_rows)
    gain = gained(x_offs, row[None], inv, pairs)
    y_offs, y_own, y_other = unless(fits, (col_offs, y_own, y_other), long_cols)
    return final(y_offs, core, gain, y_own, y_other, prior)


def solution(mesh):
    placed = (P("row", "col"), P(), P(), P(), P(), P())

    return jax.shard_map(
        local, mesh=mesh, in_specs=placed, out_specs=P("row", "col"), check_vma=False
    )
```
